1024 devices in a mesh: slab: 8 (over y), work: 128 (over z, x, core).
Axes of the slice: x: 4, y: 8, z: 16, core: 2. Of those that a mesh axis runs over, the one named last changes fastest.
Arguments:
- particles: float32 [8, 4096, 128], P(None, ('slab', 'work')), may hold values from -5 to 5, as said below
- counts: int32 [4096], P(('slab', 'work')), may hold values from 64 to 128
- partners: int32 [4096, 8], P(('slab', 'work')), may hold values from 0 to 511
Outputs:
- density: float32 [4096, 128], P(('slab', 'work'))
- acceleration: float32 [3, 4096, 128], P(None, ('slab', 'work'))
The draws below stay inside these ranges and needn't reach their ends.
Inputs may be any that keep to these rules, and one draw needn't show every extreme that they name: `particles`: rows 0 to 2 hold positions in [0, 1], rows 3 to 5 velocities in [-5, 5], row 6 smoothing lengths in [0.6, 1.2], row 7 masses in [0.0005, 0.004]. Slots from counts[g] on are empty. `partners`: partner bins lie in the bin's own slab.
All inputs are finite; a program needn't handle non-finite values.
Results may differ from the reference program's by a relative error of at most 0.00005.
Values sent between devices are 32-bit elements; how exact they have to be, the bound alone decides.
No kernel may reach another device: no remote copies, remote signals or barrier semaphores. Data moves between devices by JAX's collectives and lax.ppermute only.
A program may use at most 32 MiB of HBM per device.

```python
import jax
import jax.numpy as jnp
from jax import lax

P_SIZE = 128
K = 8
BINS_SLAB = 512
NBINS = 4096
N_SLAB = 8


def draw_particles(key, part):
    subkeys = jax.random.split(key, 6)
    grid_shape = (NBINS, P_SIZE)
    places = jax.random.uniform(subkeys[1], (3, NBINS, P_SIZE), jnp.float32)
    speeds = jnp.clip(jax.random.normal(subkeys[3], (3, NBINS, P_SIZE), jnp.float32), -5.0, 5.0)
    lengths = jnp.exp(jax.random.uniform(subkeys[4], grid_shape, jnp.float32, jnp.log(0.6), jnp.log(1.2)))
    masses = jnp.exp(jax.random.uniform(subkeys[5], grid_shape, jnp.float32, jnp.log(0.0005), jnp.log(0.004)))
    return jnp.concatenate([places, speeds, lengths[None], masses[None]], axis=0).astype(jnp.float32)


def touch_ends(values, rng, least, largest):
    shape = values.shape
    index_at = [jax.random.randint(jax.random.fold_in(rng, axis), (), 0, shape[axis]) for axis in range(len(shape))]
    values = values.at[tuple(index_at)].set(least)
    longest = shape.index(max(shape))
    index_at[longest] = (index_at[longest] + 1) % shape[longest]
    return values.at[tuple(index_at)].set(largest)


def setup_inputs(seed: int = 0) -> dict:
    key_list = jax.random.split(jax.random.key(seed), 4)
    return {
        "particles": draw_particles(jax.random.fold_in(key_list[3], 71), 0),
        "counts": touch_ends(jax.random.randint(key_list[1], (NBINS,), P_SIZE // 2, P_SIZE + 1), jax.random.fold_in(key_list[1], 1), P_SIZE // 2, P_SIZE).astype(jnp.int32),
        "partners": touch_ends(jax.random.randint(key_list[2], (NBINS, K), 0, BINS_SLAB), jax.random.fold_in(key_list[2], 1), 0, BINS_SLAB - 1).astype(jnp.int32),
    }


weight_norm = 21.0 / (16.0 * 3.141592653589793)
force_norm = 105.0 / (16.0 * 3.141592653589793)
viscosity = 0.25

def separations(pos_self, pos_other):
    offset_vec = pos_self[:, :, None] - pos_other[:, None, :]
    radius = jnp.sqrt(lax.optimization_barrier(jnp.sum(offset_vec * offset_vec, axis=0)))
    return (offset_vec, radius)

def density_sum(pos_self, len_self, pos_other, mass_other):
    offset_vec, radius = separations(pos_self, pos_other)
    scaled = radius / len_self[:, None]
    shell_val = jnp.maximum(1.0 - 0.5 * scaled, 0.0)
    kernel = shell_val ** 4 * (1.0 + 2.0 * scaled) * (weight_norm / len_self ** 3)[:, None]
    return lax.optimization_barrier(jnp.sum(kernel * mass_other[None, :], axis=1))

def force_sum(pos_self, vel_self, len_self, rho_self, pos_other, vel_other, len_other, mass_other, rho_other):
    offset_vec, radius = separations(pos_self, pos_other)
    joint_h = 0.5 * (len_self[:, None] + len_other[None, :])
    scaled = radius / joint_h
    shell_val = jnp.maximum(1.0 - 0.5 * scaled, 0.0)
    factor = force_norm * shell_val ** 3 / joint_h ** 5 * mass_other[None, :]
    pressure = factor * (1.0 / rho_self[:, None] + 1.0 / rho_other[None, :])
    damping = factor * viscosity / (rho_self[:, None] * rho_other[None, :])
    veldiff = vel_self[:, :, None] - vel_other[:, None, :]
    return lax.optimization_barrier(jnp.sum(pressure[None] * offset_vec - damping[None] * veldiff, axis=2))

def reference(particles, counts, partners):
    slot_ids = jnp.arange(P_SIZE, dtype=jnp.int32)
    filled = (slot_ids[None, :] < counts[:, None]).astype(jnp.float32)
    masked = jnp.concatenate([particles[:7], particles[7:] * filled[None]], axis=0)
    bin_ids = jnp.arange(NBINS, dtype=jnp.int32)
    slab_ids = bin_ids // BINS_SLAB
    within = bin_ids % BINS_SLAB
    lower_bin = (slab_ids + N_SLAB - 1) % N_SLAB * BINS_SLAB + within
    upper_bin = (slab_ids + 1) % N_SLAB * BINS_SLAB + within
    linked = slab_ids[:, None] * BINS_SLAB + partners
    members = jnp.concatenate([bin_ids[:, None], lower_bin[:, None], upper_bin[:, None], linked], axis=1).astype(jnp.int32)

    def density_one(bin_index):
        gathered = jnp.take(masked, members[bin_index], axis=1).reshape(8, -1)
        own_bin = masked[:, bin_index]
        return density_sum(own_bin[0:3], own_bin[6], gathered[0:3], gathered[7])
    raw_density = lax.map(density_one, bin_ids)
    safe_density = filled * raw_density + (1.0 - filled)
    density = filled * raw_density
    full_state = jnp.concatenate([masked, safe_density[None]], axis=0)

    def force_one(bin_index):
        gathered = jnp.take(full_state, members[bin_index], axis=1).reshape(9, -1)
        own_bin = full_state[:, bin_index]
        result = force_sum(own_bin[0:3], own_bin[3:6], own_bin[6], own_bin[8], gathered[0:3], gathered[3:6], gathered[6], gathered[7], gathered[8])
        return result * filled[bin_index][None]
    acceleration = lax.map(force_one, bin_ids)
    return (density, jnp.transpose(acceleration, (1, 0, 2)))
```

```python
import jax
import jax.numpy as jnp
from jax import lax
from jax.experimental import pallas as pl
from jax.experimental.pallas import tpu as pltpu
from jax.sharding import Mesh, PartitionSpec as P

weight_norm = 21.0 / (16.0 * 3.141592653589793)
force_norm = 105.0 / (16.0 * 3.141592653589793)
viscosity = 0.25

BINS = 4
LINKS = 8
SLOTS = 128
ROWS = 8
COUNT = 3 + LINKS
VMEM = pltpu.MemorySpace.VMEM
SMEM = pltpu.MemorySpace.SMEM


def locate(bin_id):
    slot = bin_id & 3
    core = (bin_id >> 2) & 1
    col = (bin_id >> 3) & 3
    layer = bin_id >> 5
    return layer, col, core, slot


def spread(rows, target, index):
    for r in range(rows.shape[0]):
        target[index, r] = jnp.broadcast_to(rows[r : r + 1, :], (8, SLOTS))


def load_members(b, partners, own, up, down, near, far, me, wide):
    spread(own[b], wide, 0)
    spread(up[b], wide, 1)
    spread(down[b], wide, 2)
    for k in range(LINKS):
        layer, col, core, slot = locate(partners[b, k])
        index = (col * 16 + layer) * BINS + slot
        tile = jnp.where(core == me, near[index], far[index])
        spread(tile, wide, 3 + k)


def density_kernel(partners, counts, own, up, down, near, far, raw_out, den_out, rho_out, wide, tall, acc):
    me = lax.axis_index("core")

    def per_bin(b, carry):
        load_members(b, partners, own, up, down, near, far, me, wide)
        tall[...] = own[b].T

        def per_chunk(c, carry):
            start = pl.multiple_of(c * 8, 8)
            cols = tall[pl.ds(start, 8), :]
            xi, yi, zi, hi = (jnp.broadcast_to(cols[:, r : r + 1], (8, SLOTS)) for r in (0, 1, 2, 6))
            inv = 0.5 / hi
            total = jnp.zeros((8, SLOTS), jnp.float32)
            for j in range(COUNT):
                dx = xi - wide[j, 0]
                dy = yi - wide[j, 1]
                dz = zi - wide[j, 2]
                half = jnp.sqrt(dx * dx + dy * dy + dz * dz) * inv
                s = jnp.maximum(1.0 - half, 0.0)
                s2 = s * s
                total = total + (s2 * s2) * (1.0 + 4.0 * half) * wide[j, 7]
            acc[pl.ds(start, 8), :] = total * (weight_norm / (hi * hi * hi))
            return carry

        lax.fori_loop(0, SLOTS // 8, per_chunk, 0)
        raw = jnp.sum(acc[...].T, axis=0, keepdims=True)
        lane = lax.broadcasted_iota(jnp.int32, (1, SLOTS), 1)
        filled = (lane < counts[b]).astype(jnp.float32)
        den_out[pl.ds(b, 1), :] = filled * raw
        rho_out[pl.ds(b, 1), :] = filled * raw + (1.0 - filled)
        return carry

    lax.fori_loop(0, BINS, per_bin, 0)


def force_kernel(
    partners, counts, own, up, down, near, far, rho, rho_up, rho_down, rho_near, rho_far, out, wide, wide_rho, tall, tall_rho, acc
):
    me = lax.axis_index("core")

    def per_bin(b, carry):
        load_members(b, partners, own, up, down, near, far, me, wide)
        row = pl.ds(b, 1)
        for j, ref in enumerate((rho, rho_up, rho_down)):
            wide_rho[j] = jnp.broadcast_to(1.0 / ref[row, :], (8, SLOTS))
        for k in range(LINKS):
            layer, col, core, slot = locate(partners[b, k])
            at = pl.ds((layer * 4 + col) * BINS + slot, 1)
            value = jnp.where(core == me, rho_near[at, :], rho_far[at, :])
            wide_rho[3 + k] = jnp.broadcast_to(1.0 / value, (8, SLOTS))
        tall[...] = own[b].T
        tall_rho[...] = wide_rho[0].T

        def per_chunk(c, carry):
            start = pl.multiple_of(c * 8, 8)
            cols = tall[pl.ds(start, 8), :]
            xi, yi, zi, ui, vi, wi, hi = (jnp.broadcast_to(cols[:, r : r + 1], (8, SLOTS)) for r in range(7))
            di = jnp.broadcast_to(tall_rho[pl.ds(start, 8), :][:, 0:1], (8, SLOTS))
            drag = viscosity * di
            ax = jnp.zeros((8, SLOTS), jnp.float32)
            ay, az = ax, ax
            for j in range(COUNT):
                dx = xi - wide[j, 0]
                dy = yi - wide[j, 1]
                dz = zi - wide[j, 2]
                radius = jnp.sqrt(dx * dx + dy * dy + dz * dz)
                inv = 1.0 / (hi + wide[j, 6])
                s = jnp.maximum(1.0 - radius * inv, 0.0) * inv
                dj = wide_rho[j]
                factor = (s * s * s) * (inv * inv) * wide[j, 7]
                push = factor * (di + dj)
                damp = factor * dj * drag
                ax = ax + (push * dx - damp * (ui - wide[j, 3]))
                ay = ay + (push * dy - damp * (vi - wide[j, 4]))
                az = az + (push * dz - damp * (wi - wide[j, 5]))
            acc[0, pl.ds(start, 8), :] = ax
            acc[1, pl.ds(start, 8), :] = ay
            acc[2, pl.ds(start, 8), :] = az
            return carry

        lax.fori_loop(0, SLOTS // 8, per_chunk, 0)
        lane = lax.broadcasted_iota(jnp.int32, (1, SLOTS), 1)
        scale = (lane < counts[b]).astype(jnp.float32) * (32.0 * force_norm)
        for d in range(3):
            out[d, row, :] = jnp.sum(acc[d].T, axis=0, keepdims=True) * scale
        return carry

    lax.fori_loop(0, BINS, per_bin, 0)


def both_ways(value):
    count = lax.axis_size("slab")
    up = [(i, (i + 1) % count) for i in range(count)]
    down = [(j, i) for i, j in up]
    return lax.ppermute(value, "slab", up), lax.ppermute(value, "slab", down)


def exchange(block, axis):
    count = lax.axis_size(axis)
    return lax.all_to_all(jnp.broadcast_to(block[None], (count,) + block.shape), axis, 0, 0, tiled=True)


def other_core(value):
    return lax.ppermute(value, "core", [(0, 1), (1, 0)])


def per_device(particles, counts, partners):
    filled = (jnp.arange(SLOTS, dtype=jnp.int32)[None, :] < counts[:, None]).astype(jnp.float32)
    masked = jnp.concatenate([particles[:7], particles[7:] * filled[None]], axis=0)
    own = jnp.transpose(masked, (1, 0, 2))
    up, down = both_ways(own)
    column = exchange(own, "z")
    near = exchange(column, "x").reshape(-1, ROWS, SLOTS)
    far = other_core(near)
    f32 = jnp.float32
    smem, vmem = pl.BlockSpec(memory_space=SMEM), pl.BlockSpec(memory_space=VMEM)
    row_shape = jax.ShapeDtypeStruct((BINS, SLOTS), f32)
    density, rho = pl.pallas_call(
        lambda p, c, o, u, d, n, f, den, rh, *scratch: density_kernel(p, c, o, u, d, n, f, None, den, rh, *scratch),
        out_shape=(row_shape, row_shape),
        in_specs=[smem, smem] + [vmem] * 5,
        out_specs=(vmem, vmem),
        scratch_shapes=[
            pltpu.VMEM((COUNT, ROWS, 8, SLOTS), f32),
            pltpu.VMEM((SLOTS, ROWS), f32),
            pltpu.VMEM((SLOTS, SLOTS), f32),
        ],
        name="density",
    )(partners, counts, own, up, down, near, far)
    rho_up, rho_down = both_ways(rho)
    rho_near = exchange(rho, ("z", "x")).reshape(-1, SLOTS)
    rho_far = other_core(rho_near)
    acceleration = pl.pallas_call(
        force_kernel,
        out_shape=jax.ShapeDtypeStruct((3, BINS, SLOTS), f32),
        in_specs=[smem, smem] + [vmem] * 10,
        out_specs=vmem,
        scratch_shapes=[
            pltpu.VMEM((COUNT, ROWS, 8, SLOTS), f32),
            pltpu.VMEM((COUNT, 8, SLOTS), f32),
            pltpu.VMEM((SLOTS, ROWS), f32),
            pltpu.VMEM((SLOTS, 8), f32),
            pltpu.VMEM((3, SLOTS, SLOTS), f32),
        ],
        name="force",
    )(partners, counts, own, up, down, near, far, rho, rho_up, rho_down, rho_near, rho_far)
    return density, acceleration


def solution(mesh):
    grid = Mesh(mesh.devices.reshape(mesh.shape["slab"], 16, 4, 2), ("slab", "z", "x", "core"))
    axes = ("slab", "z", "x", "core")
    return jax.shard_map(
        per_device,
        mesh=grid,
        in_specs=(P(None, axes, None), P(axes), P(axes, None)),
        out_specs=(P(axes, None), P(None, axes, None)),
        check_vma=False,
    )
```

```python
import jax
import jax.numpy as jnp
from jax import lax
from jax.experimental import pallas as pl
from jax.experimental.pallas import tpu as pltpu
from jax.sharding import Mesh, PartitionSpec as P

weight_norm = 21.0 / (16.0 * 3.141592653589793)
force_norm = 105.0 / (16.0 * 3.141592653589793)
viscosity = 0.25

BINS = 4
LINKS = 8
SLOTS = 128
ROWS = 8
COUNT = 3 + LINKS
CHUNKS = SLOTS // 8
F32 = jnp.float32
VMEM = pl.BlockSpec(memory_space=pltpu.MemorySpace.VMEM)
SMEM = pl.BlockSpec(memory_space=pltpu.MemorySpace.SMEM)
ANY = pl.BlockSpec(memory_space=pl.ANY)


def shape(*dims):
    return jax.ShapeDtypeStruct(dims, F32)


def root(square):
    return square * lax.rsqrt(jnp.maximum(square, 1e-36))


def columns(tall, c, rows):
    cols = tall[c * 8 : c * 8 + 8, :]
    return [jnp.broadcast_to(cols[:, r : r + 1], (8, SLOTS)) for r in rows]


def density_terms(tall, others, acc):
    for c in range(CHUNKS):
        xi, yi, zi, hi = columns(tall, c, (0, 1, 2, 6))
        inv = 0.5 / hi
        total = jnp.zeros((8, SLOTS), F32)
        for row in others:
            dx = xi - row(0)
            dy = yi - row(1)
            dz = zi - row(2)
            s = jnp.maximum(1.0 - root(dx * dx + dy * dy + dz * dz) * inv, 0.0)
            s2 = s * s
            total = total + (s2 * s2) * (5.0 - 4.0 * s) * row(7)
        acc[c * 8 : c * 8 + 8, :] = total * (weight_norm / (hi * hi * hi))
    return jnp.sum(acc[...].T, axis=0, keepdims=True)


def reader(ref, *index):
    return lambda r: ref[(*index, pl.ds(r, 8, stride=0), slice(None))]


def near_density_kernel(own, up, down, out, tall, acc):
    def per_bin(b, carry):
        tall[...] = own[b].T
        out[pl.ds(b, 1), :] = density_terms(tall, [reader(ref, b) for ref in (own, up, down)], acc)
        return carry

    lax.fori_loop(0, BINS, per_bin, 0)


def partner_density_kernel(partners, counts, own, part, near, far, den_out, inv_out, members, tall, acc, sems):
    me = lax.axis_index("core")

    def copies(b, k):
        bin_id = partners[b, k]
        index = (((bin_id >> 3) & 3) * 16 + (bin_id >> 5)) * BINS + (bin_id & 3)
        at = b * LINKS + k
        mine = ((bin_id >> 2) & 1) == me
        return mine, [pltpu.make_async_copy(ref.at[index], members.at[at], sems.at[at]) for ref in (near, far)]

    for b in range(BINS):
        for k in range(LINKS):
            mine, (from_near, from_far) = copies(b, k)
            pl.when(mine)(from_near.start)
            pl.when(jnp.logical_not(mine))(from_far.start)

    def per_bin(b, carry):
        tall[...] = own[b].T
        for k in range(LINKS):
            at = b * LINKS + k
            pltpu.make_async_copy(near.at[0], members.at[at], sems.at[at]).wait()
        far_part = density_terms(tall, [reader(members, b * LINKS + k) for k in range(LINKS)], acc)
        raw = part[pl.ds(b, 1), :] + far_part
        lane = lax.broadcasted_iota(jnp.int32, (1, SLOTS), 1)
        filled = (lane < counts[b]).astype(F32)
        den_out[pl.ds(b, 1), :] = filled * raw
        inv_out[pl.ds(b, 1), :] = 1.0 / (filled * raw + (1.0 - filled))
        return carry

    lax.fori_loop(0, BINS, per_bin, 0)


def factor_kernel(own, up, down, members, out, base, tall, acc):
    tall[...] = own[0].T
    others = [reader(ref, 0) for ref in (own, up, down)] + [reader(members, k) for k in range(LINKS)]
    for c in range(CHUNKS):
        xi, yi, zi, hi = columns(tall, c, (0, 1, 2, 6))
        ax = jnp.zeros((8, SLOTS), F32)
        ay, az = ax, ax
        for j, row in enumerate(others):
            dx = xi - row(0)
            dy = yi - row(1)
            dz = zi - row(2)
            inv = 1.0 / (hi + row(6))
            s = jnp.maximum(1.0 - root(dx * dx + dy * dy + dz * dz) * inv, 0.0) * inv
            factor = (s * s * s) * (inv * inv) * row(7)
            out[0, j, c * 8 : c * 8 + 8, :] = factor
            ax = ax + factor * dx
            ay = ay + factor * dy
            az = az + factor * dz
        for d, total in enumerate((ax, ay, az)):
            acc[d, c * 8 : c * 8 + 8, :] = total
    for d in range(3):
        base[0, d : d + 1, :] = jnp.sum(acc[d].T, axis=0, keepdims=True)


def force_kernel(partners, counts, own, up, down, members, factors, base, mine, mine_up, mine_down, inverse, out, weights, tall, acc):
    b = pl.program_id(0)
    for j, ref in enumerate((mine, mine_up, mine_down)):
        weights[j : j + 1, :] = ref[pl.ds(b, 1), :]
    for k in range(LINKS):
        weights[3 + k : 4 + k, :] = inverse[pl.ds(partners[b, k], 1), :]
    tall[...] = own[0].T
    others = [reader(ref, 0) for ref in (own, up, down)] + [reader(members, k) for k in range(LINKS)]
    for c in range(CHUNKS):
        xi, yi, zi, ui, vi, wi = columns(tall, c, range(6))
        ax = jnp.zeros((8, SLOTS), F32)
        ay, az, bx, by, bz = (ax,) * 5
        for j, row in enumerate(others):
            factor = factors[0, j, c * 8 : c * 8 + 8, :] * weights[pl.ds(j, 8, stride=0), :]
            ax = ax + factor * (xi - row(0))
            ay = ay + factor * (yi - row(1))
            az = az + factor * (zi - row(2))
            bx = bx + factor * (ui - row(3))
            by = by + factor * (vi - row(4))
            bz = bz + factor * (wi - row(5))
        for d, total in enumerate((ax, ay, az, bx, by, bz)):
            acc[d, c * 8 : c * 8 + 8, :] = total
    lane = lax.broadcasted_iota(jnp.int32, (1, SLOTS), 1)
    scale = (lane < counts[b]).astype(F32) * (32.0 * force_norm)
    weight = weights[0:1, :]
    for d in range(3):
        push = jnp.sum(acc[d].T, axis=0, keepdims=True)
        drag = jnp.sum(acc[3 + d].T, axis=0, keepdims=True)
        out[0, d : d + 1, :] = (push + weight * (base[0, d : d + 1, :] - viscosity * drag)) * scale


def both_ways(value):
    count = lax.axis_size("slab")
    up = [(i, (i + 1) % count) for i in range(count)]
    down = [(j, i) for i, j in up]
    return lax.ppermute(value, "slab", up), lax.ppermute(value, "slab", down)


def exchange(block, axis):
    count = lax.axis_size(axis)
    return lax.all_to_all(jnp.broadcast_to(block[None], (count,) + block.shape), axis, 0, 0, tiled=True)


def cost(pairs, ops):
    work = pairs * SLOTS * SLOTS
    return pl.CostEstimate(flops=work * ops, bytes_accessed=work * 4, transcendentals=work)


def limit(mib):
    return pltpu.CompilerParams(vmem_limit_bytes=mib << 20)


def per_device(particles, counts, partners):
    filled = (jnp.arange(SLOTS, dtype=jnp.int32)[None, :] < counts[:, None]).astype(F32)
    masked = jnp.concatenate([particles[:7], particles[7:] * filled[None]], axis=0)
    own = jnp.transpose(masked, (1, 0, 2))
    up, down = both_ways(own)
    column = exchange(own, "z")
    work_scratch = [pltpu.VMEM((SLOTS, ROWS), F32), pltpu.VMEM((SLOTS, SLOTS), F32)]
    part = pl.pallas_call(
        near_density_kernel,
        out_shape=shape(BINS, SLOTS),
        in_specs=[VMEM] * 3,
        out_specs=VMEM,
        scratch_shapes=work_scratch,
        cost_estimate=cost(3 * BINS, 20),
        compiler_params=limit(8),
        name="near_density",
    )(own, up, down)
    column, part = lax.optimization_barrier((column, part))
    near = exchange(column, "x").reshape(-1, ROWS, SLOTS)
    far = lax.ppermute(near, "core", [(0, 1), (1, 0)])
    density, mine, members = pl.pallas_call(
        partner_density_kernel,
        out_shape=(shape(BINS, SLOTS), shape(BINS, SLOTS), shape(BINS * LINKS, ROWS, SLOTS)),
        in_specs=[SMEM, SMEM, VMEM, VMEM, ANY, ANY],
        out_specs=(VMEM, VMEM, VMEM),
        scratch_shapes=work_scratch + [pltpu.SemaphoreType.DMA((BINS * LINKS,))],
        cost_estimate=cost(LINKS * BINS, 20),
        compiler_params=limit(8),
        name="partner_density",
    )(partners, counts, own, part, near, far)
    mine_up, mine_down = both_ways(mine)
    inverse = exchange(mine, ("z", "x", "core")).reshape(-1, SLOTS)
    tile = pl.BlockSpec((1, ROWS, SLOTS), lambda b: (b, 0, 0))
    links = pl.BlockSpec((LINKS, ROWS, SLOTS), lambda b: (b, 0, 0))
    pairs = pl.BlockSpec((1, COUNT, SLOTS, SLOTS), lambda b: (b, 0, 0, 0))
    vector = pl.BlockSpec((1, 3, SLOTS), lambda b: (b, 0, 0))
    factors, base = pl.pallas_call(
        factor_kernel,
        grid=(BINS,),
        out_shape=(shape(BINS, COUNT, SLOTS, SLOTS), shape(BINS, 3, SLOTS)),
        in_specs=[tile, tile, tile, links],
        out_specs=(pairs, vector),
        scratch_shapes=[pltpu.VMEM((SLOTS, ROWS), F32), pltpu.VMEM((3, SLOTS, SLOTS), F32)],
        cost_estimate=cost(COUNT * BINS, 40),
        compiler_params=limit(8),
        name="factor",
    )(own, up, down, members)
    acceleration = pl.pallas_call(
        force_kernel,
        grid=(BINS,),
        out_shape=shape(BINS, 3, SLOTS),
        in_specs=[SMEM, SMEM, tile, tile, tile, links, pairs, vector, VMEM, VMEM, VMEM, VMEM],
        out_specs=vector,
        scratch_shapes=[
            pltpu.VMEM((16, SLOTS), F32),
            pltpu.VMEM((SLOTS, ROWS), F32),
            pltpu.VMEM((6, SLOTS, SLOTS), F32),
        ],
        cost_estimate=cost(COUNT * BINS, 20),
        compiler_params=limit(8),
        name="force",
    )(partners, counts, own, up, down, members, factors, base, mine, mine_up, mine_down, inverse)
    return density, jnp.transpose(acceleration, (1, 0, 2))


def solution(mesh):
    grid = Mesh(mesh.devices.reshape(mesh.shape["slab"], 16, 4, 2), ("slab", "z", "x", "core"))
    axes = ("slab", "z", "x", "core")
    return jax.shard_map(
        per_device,
        mesh=grid,
        in_specs=(P(None, axes, None), P(axes), P(axes, None)),
        out_specs=(P(axes, None), P(None, axes, None)),
        check_vma=False,
    )
```

```python
import jax
import jax.numpy as jnp
from jax import lax
from jax.experimental import pallas as pl
from jax.experimental.pallas import tpu as pltpu
from jax.sharding import Mesh, PartitionSpec as P

weight_norm = 21.0 / (16.0 * 3.141592653589793)
force_norm = 105.0 / (16.0 * 3.141592653589793)
viscosity = 0.25

BINS = 4
LINKS = 8
SLOTS = 128
ROWS = 8
COUNT = 3 + LINKS
CHUNKS = SLOTS // 8
F32 = jnp.float32
VMEM = pl.BlockSpec(memory_space=pltpu.MemorySpace.VMEM)
SMEM = pl.BlockSpec(memory_space=pltpu.MemorySpace.SMEM)
ANY = pl.BlockSpec(memory_space=pl.ANY)


def shape(*dims):
    return jax.ShapeDtypeStruct(dims, F32)


def root(square):
    return square * lax.rsqrt(jnp.maximum(square, 1e-36))


def columns(tall, c, rows):
    cols = tall[c * 8 : c * 8 + 8, :]
    return [jnp.broadcast_to(cols[:, r : r + 1], (8, SLOTS)) for r in rows]


def density_terms(tall, others, acc):
    for c in range(CHUNKS):
        xi, yi, zi, hi = columns(tall, c, (0, 1, 2, 6))
        inv = 0.5 / hi
        total = jnp.zeros((8, SLOTS), F32)
        for row in others:
            dx = xi - row(0)
            dy = yi - row(1)
            dz = zi - row(2)
            s = jnp.maximum(1.0 - root(dx * dx + dy * dy + dz * dz) * inv, 0.0)
            s2 = s * s
            total = total + (s2 * s2) * (5.0 - 4.0 * s) * row(7)
        acc[c * 8 : c * 8 + 8, :] = total * (weight_norm / (hi * hi * hi))
    return jnp.sum(acc[...].T, axis=0, keepdims=True)


def reader(ref, *index):
    return lambda r: ref[(*index, pl.ds(r, 8, stride=0), slice(None))]


def near_density_kernel(own, up, down, out, tall, acc):
    def per_bin(b, carry):
        tall[...] = own[b].T
        out[pl.ds(b, 1), :] = density_terms(tall, [reader(ref, b) for ref in (own, up, down)], acc)
        return carry

    lax.fori_loop(0, BINS, per_bin, 0)


def partner_density_kernel(partners, counts, own, part, near, far, den_out, inv_out, members, tall, acc, sems):
    me = lax.axis_index("core")

    def copies(b, k):
        bin_id = partners[b, k]
        index = (((bin_id >> 3) & 3) * 16 + (bin_id >> 5)) * BINS + (bin_id & 3)
        at = b * LINKS + k
        mine = ((bin_id >> 2) & 1) == me
        return mine, [pltpu.make_async_copy(ref.at[index], members.at[at], sems.at[at]) for ref in (near, far)]

    for b in range(BINS):
        for k in range(LINKS):
            mine, (from_near, from_far) = copies(b, k)
            pl.when(mine)(from_near.start)
            pl.when(jnp.logical_not(mine))(from_far.start)

    def per_bin(b, carry):
        tall[...] = own[b].T
        for k in range(LINKS):
            at = b * LINKS + k
            pltpu.make_async_copy(near.at[0], members.at[at], sems.at[at]).wait()
        far_part = density_terms(tall, [reader(members, b * LINKS + k) for k in range(LINKS)], acc)
        raw = part[pl.ds(b, 1), :] + far_part
        lane = lax.broadcasted_iota(jnp.int32, (1, SLOTS), 1)
        filled = (lane < counts[b]).astype(F32)
        den_out[pl.ds(b, 1), :] = filled * raw
        inv_out[pl.ds(b, 1), :] = 1.0 / (filled * raw + (1.0 - filled))
        return carry

    lax.fori_loop(0, BINS, per_bin, 0)


def factor_kernel(own, up, down, members, out, base, tall, acc):
    tall[...] = own[0].T
    others = [reader(ref, 0) for ref in (own, up, down)] + [reader(members, k) for k in range(LINKS)]
    for c in range(CHUNKS):
        xi, yi, zi, hi = columns(tall, c, (0, 1, 2, 6))
        ax = jnp.zeros((8, SLOTS), F32)
        ay, az = ax, ax
        for j, row in enumerate(others):
            dx = xi - row(0)
            dy = yi - row(1)
            dz = zi - row(2)
            inv = 1.0 / (hi + row(6))
            s = jnp.maximum(1.0 - root(dx * dx + dy * dy + dz * dz) * inv, 0.0) * inv
            factor = (s * s * s) * (inv * inv) * row(7)
            out[0, j, c * 8 : c * 8 + 8, :] = factor
            ax = ax + factor * dx
            ay = ay + factor * dy
            az = az + factor * dz
        for d, total in enumerate((ax, ay, az)):
            acc[d, c * 8 : c * 8 + 8, :] = total
    for d in range(3):
        base[0, d : d + 1, :] = jnp.sum(acc[d].T, axis=0, keepdims=True)


def force_kernel(partners, counts, own, up, down, members, factors, base, mine, mine_up, mine_down, inverse, out, weights, tall, acc):
    b = pl.program_id(0)
    for j, ref in enumerate((mine, mine_up, mine_down)):
        weights[j : j + 1, :] = ref[pl.ds(b, 1), :]
    for k in range(LINKS):
        bin_id = partners[b, k]
        at = (((bin_id >> 2) & 7) * 16 + (bin_id >> 5)) * BINS + (bin_id & 3)
        weights[3 + k : 4 + k, :] = inverse[pl.ds(at, 1), :]
    tall[...] = own[0].T
    others = [reader(ref, 0) for ref in (own, up, down)] + [reader(members, k) for k in range(LINKS)]
    for c in range(CHUNKS):
        xi, yi, zi, ui, vi, wi = columns(tall, c, range(6))
        ax = jnp.zeros((8, SLOTS), F32)
        ay, az, bx, by, bz = (ax,) * 5
        for j, row in enumerate(others):
            factor = factors[0, j, c * 8 : c * 8 + 8, :] * weights[pl.ds(j, 8, stride=0), :]
            ax = ax + factor * (xi - row(0))
            ay = ay + factor * (yi - row(1))
            az = az + factor * (zi - row(2))
            bx = bx + factor * (ui - row(3))
            by = by + factor * (vi - row(4))
            bz = bz + factor * (wi - row(5))
        for d, total in enumerate((ax, ay, az, bx, by, bz)):
            acc[d, c * 8 : c * 8 + 8, :] = total
    lane = lax.broadcasted_iota(jnp.int32, (1, SLOTS), 1)
    scale = (lane < counts[b]).astype(F32) * (32.0 * force_norm)
    weight = weights[0:1, :]
    for d in range(3):
        push = jnp.sum(acc[d].T, axis=0, keepdims=True)
        drag = jnp.sum(acc[3 + d].T, axis=0, keepdims=True)
        out[0, d : d + 1, :] = (push + weight * (base[0, d : d + 1, :] - viscosity * drag)) * scale


def both_ways(value):
    count = lax.axis_size("slab")
    up = [(i, (i + 1) % count) for i in range(count)]
    down = [(j, i) for i, j in up]
    return lax.ppermute(value, "slab", up), lax.ppermute(value, "slab", down)


def exchange(block, axis):
    count = lax.axis_size(axis)
    return lax.all_to_all(jnp.broadcast_to(block[None], (count,) + block.shape), axis, 0, 0, tiled=True)


def cost(pairs, ops):
    work = pairs * SLOTS * SLOTS
    return pl.CostEstimate(flops=work * ops, bytes_accessed=work * 4, transcendentals=work)


def limit(mib):
    return pltpu.CompilerParams(vmem_limit_bytes=mib << 20)


def per_device(particles, counts, partners):
    filled = (jnp.arange(SLOTS, dtype=jnp.int32)[None, :] < counts[:, None]).astype(F32)
    masked = jnp.concatenate([particles[:7], particles[7:] * filled[None]], axis=0)
    own = jnp.transpose(masked, (1, 0, 2))
    up, down = both_ways(own)
    column = exchange(own, "z")
    work_scratch = [pltpu.VMEM((SLOTS, ROWS), F32), pltpu.VMEM((SLOTS, SLOTS), F32)]
    part = pl.pallas_call(
        near_density_kernel,
        out_shape=shape(BINS, SLOTS),
        in_specs=[VMEM] * 3,
        out_specs=VMEM,
        scratch_shapes=work_scratch,
        cost_estimate=cost(3 * BINS, 20),
        compiler_params=limit(8),
        name="near_density",
    )(own, up, down)
    column, part = lax.optimization_barrier((column, part))
    near = exchange(column, "x").reshape(-1, ROWS, SLOTS)
    far = lax.ppermute(near, "core", [(0, 1), (1, 0)])
    density, mine, members = pl.pallas_call(
        partner_density_kernel,
        out_shape=(shape(BINS, SLOTS), shape(BINS, SLOTS), shape(BINS * LINKS, ROWS, SLOTS)),
        in_specs=[SMEM, SMEM, VMEM, VMEM, ANY, ANY],
        out_specs=(VMEM, VMEM, VMEM),
        scratch_shapes=work_scratch + [pltpu.SemaphoreType.DMA((BINS * LINKS,))],
        cost_estimate=cost(LINKS * BINS, 20),
        compiler_params=limit(8),
        name="partner_density",
    )(partners, counts, own, part, near, far)
    mine_up, mine_down = both_ways(mine)
    layer = exchange(mine, "z")
    tile = pl.BlockSpec((1, ROWS, SLOTS), lambda b: (b, 0, 0))
    links = pl.BlockSpec((LINKS, ROWS, SLOTS), lambda b: (b, 0, 0))
    pairs = pl.BlockSpec((1, COUNT, SLOTS, SLOTS), lambda b: (b, 0, 0, 0))
    vector = pl.BlockSpec((1, 3, SLOTS), lambda b: (b, 0, 0))
    factors, base = pl.pallas_call(
        factor_kernel,
        grid=(BINS,),
        out_shape=(shape(BINS, COUNT, SLOTS, SLOTS), shape(BINS, 3, SLOTS)),
        in_specs=[tile, tile, tile, links],
        out_specs=(pairs, vector),
        scratch_shapes=[pltpu.VMEM((SLOTS, ROWS), F32), pltpu.VMEM((3, SLOTS, SLOTS), F32)],
        cost_estimate=cost(COUNT * BINS, 40),
        compiler_params=limit(8),
        name="factor",
    )(own, up, down, members)
    layer, base, mine_up, mine_down = lax.optimization_barrier((layer, base, mine_up, mine_down))
    inverse = exchange(layer, ("x", "core")).reshape(-1, SLOTS)
    acceleration = pl.pallas_call(
        force_kernel,
        grid=(BINS,),
        out_shape=shape(BINS, 3, SLOTS),
        in_specs=[SMEM, SMEM, tile, tile, tile, links, pairs, vector, VMEM, VMEM, VMEM, VMEM],
        out_specs=vector,
        scratch_shapes=[
            pltpu.VMEM((16, SLOTS), F32),
            pltpu.VMEM((SLOTS, ROWS), F32),
            pltpu.VMEM((6, SLOTS, SLOTS), F32),
        ],
        cost_estimate=cost(COUNT * BINS, 20),
        compiler_params=limit(8),
        name="force",
    )(partners, counts, own, up, down, members, factors, base, mine, mine_up, mine_down, inverse)
    return density, jnp.transpose(acceleration, (1, 0, 2))


def solution(mesh):
    grid = Mesh(mesh.devices.reshape(mesh.shape["slab"], 16, 4, 2), ("slab", "z", "x", "core"))
    axes = ("slab", "z", "x", "core")
    return jax.shard_map(
        per_device,
        mesh=grid,
        in_specs=(P(None, axes, None), P(axes), P(axes, None)),
        out_specs=(P(axes, None), P(None, axes, None)),
        check_vma=False,
    )
```

```python
import jax
import jax.numpy as jnp
from jax import lax
from jax.experimental import pallas as pl
from jax.experimental.pallas import tpu as pltpu
from jax.sharding import Mesh, PartitionSpec as P

weight_norm = 21.0 / (16.0 * 3.141592653589793)
force_norm = 105.0 / (16.0 * 3.141592653589793)
viscosity = 0.25

BINS = 4
LINKS = 8
SLOTS = 128
ROWS = 8
COUNT = 3 + LINKS
CHUNKS = SLOTS // 8
F32 = jnp.float32
VMEM = pl.BlockSpec(memory_space=pltpu.MemorySpace.VMEM)
SMEM = pl.BlockSpec(memory_space=pltpu.MemorySpace.SMEM)
ANY = pl.BlockSpec(memory_space=pl.ANY)


def shape(*dims):
    return jax.ShapeDtypeStruct(dims, F32)


def root(square):
    return square * lax.rsqrt(jnp.maximum(square, 1e-36))


def columns(tall, c, rows):
    cols = tall[c * 8 : c * 8 + 8, :]
    return [jnp.broadcast_to(cols[:, r : r + 1], (8, SLOTS)) for r in rows]


def density_terms(tall, others, acc):
    for c in range(CHUNKS):
        xi, yi, zi, hi = columns(tall, c, (0, 1, 2, 6))
        inv = 0.5 / hi
        total = jnp.zeros((8, SLOTS), F32)
        for row in others:
            dx = xi - row(0)
            dy = yi - row(1)
            dz = zi - row(2)
            s = jnp.maximum(1.0 - root(dx * dx + dy * dy + dz * dz) * inv, 0.0)
            s2 = s * s
            total = total + (s2 * s2) * (5.0 - 4.0 * s) * row(7)
        acc[c * 8 : c * 8 + 8, :] = total * (weight_norm / (hi * hi * hi))
    return jnp.sum(acc[...].T, axis=0, keepdims=True)


def reader(ref, *index):
    return lambda r: ref[(*index, pl.ds(r, 8, stride=0), slice(None))]


def prepare_kernel(counts, particles, own, block):
    lane = lax.broadcasted_iota(jnp.int32, (1, SLOTS), 1)
    for b in range(BINS):
        filled = (lane < counts[b]).astype(F32)
        for r in range(ROWS):
            row = particles[r, b : b + 1, :]
            own[b, r : r + 1, :] = row * filled if r == 7 else row
        tile = own[b]
        for copy in range(block.shape[0]):
            block[copy, b] = tile


def factor_terms(tall, others, store, acc):
    for c in range(CHUNKS):
        xi, yi, zi, hi = columns(tall, c, (0, 1, 2, 6))
        ax = jnp.zeros((8, SLOTS), F32)
        ay, az = ax, ax
        for j, row in enumerate(others):
            dx = xi - row(0)
            dy = yi - row(1)
            dz = zi - row(2)
            inv = 1.0 / (hi + row(6))
            s = jnp.maximum(1.0 - root(dx * dx + dy * dy + dz * dz) * inv, 0.0) * inv
            factor = (s * s * s) * (inv * inv) * row(7)
            store[0, j, c * 8 : c * 8 + 8, :] = factor
            ax = ax + factor * dx
            ay = ay + factor * dy
            az = az + factor * dz
        for d, total in enumerate((ax, ay, az)):
            acc[d, c * 8 : c * 8 + 8, :] = total
    return [jnp.sum(acc[d].T, axis=0, keepdims=True) for d in range(3)]


def near_kernel(own, up, down, part, factors, base, tall, acc, acc3):
    tall[...] = own[0].T
    others = [reader(ref, 0) for ref in (own, up, down)]
    part[0] = density_terms(tall, others, acc)
    for d, total in enumerate(factor_terms(tall, others, factors, acc3)):
        base[0, d : d + 1, :] = total


def partner_density_kernel(partners, counts, own, part, near, far, den_out, inv_out, block, members, tall, acc, sems):
    me = lax.axis_index("core")

    def copies(b, k):
        bin_id = partners[b, k]
        index = (((bin_id >> 3) & 3) * 16 + (bin_id >> 5)) * BINS + (bin_id & 3)
        at = b * LINKS + k
        mine = ((bin_id >> 2) & 1) == me
        return mine, [pltpu.make_async_copy(ref.at[index], members.at[at], sems.at[at]) for ref in (near, far)]

    for b in range(BINS):
        for k in range(LINKS):
            mine, (from_near, from_far) = copies(b, k)
            pl.when(mine)(from_near.start)
            pl.when(jnp.logical_not(mine))(from_far.start)

    def per_bin(b, carry):
        tall[...] = own[b].T
        for k in range(LINKS):
            at = b * LINKS + k
            pltpu.make_async_copy(near.at[0], members.at[at], sems.at[at]).wait()
        far_part = density_terms(tall, [reader(members, b * LINKS + k) for k in range(LINKS)], acc)
        raw = part[b] + far_part
        lane = lax.broadcasted_iota(jnp.int32, (1, SLOTS), 1)
        filled = (lane < counts[b]).astype(F32)
        den_out[pl.ds(b, 1), :] = filled * raw
        inv_out[pl.ds(b, 1), :] = 1.0 / (filled * raw + (1.0 - filled))
        return carry

    lax.fori_loop(0, BINS, per_bin, 0)
    inverse = inv_out[...]
    for copy in range(block.shape[0]):
        block[copy] = inverse


def factor_kernel(own, members, factors, base, tall, acc3):
    tall[...] = own[0].T
    for d, total in enumerate(factor_terms(tall, [reader(members, k) for k in range(LINKS)], factors, acc3)):
        base[0, d : d + 1, :] = total


def force_kernel(
    partners,
    counts,
    own,
    up,
    down,
    members,
    near_factors,
    far_factors,
    near_base,
    far_base,
    mine,
    mine_up,
    mine_down,
    inverse,
    out,
    weights,
    tall,
    acc,
):
    b = pl.program_id(0)
    for j, ref in enumerate((mine, mine_up, mine_down)):
        weights[j : j + 1, :] = ref[pl.ds(b, 1), :]
    for k in range(LINKS):
        bin_id = partners[b, k]
        at = ((bin_id >> 2) & 1) * 256 + (bin_id >> 3) * BINS + (bin_id & 3)
        weights[3 + k : 4 + k, :] = inverse[pl.ds(at, 1), :]
    tall[...] = own[0].T
    others = [(reader(ref, 0), near_factors, j) for j, ref in enumerate((own, up, down))]
    others += [(reader(members, k), far_factors, k) for k in range(LINKS)]
    for c in range(CHUNKS):
        xi, yi, zi, ui, vi, wi = columns(tall, c, range(6))
        ax = jnp.zeros((8, SLOTS), F32)
        ay, az, bx, by, bz = (ax,) * 5
        for j, (row, factors, at) in enumerate(others):
            factor = factors[0, at, c * 8 : c * 8 + 8, :] * weights[pl.ds(j, 8, stride=0), :]
            ax = ax + factor * (xi - row(0))
            ay = ay + factor * (yi - row(1))
            az = az + factor * (zi - row(2))
            bx = bx + factor * (ui - row(3))
            by = by + factor * (vi - row(4))
            bz = bz + factor * (wi - row(5))
        for d, total in enumerate((ax, ay, az, bx, by, bz)):
            acc[d, c * 8 : c * 8 + 8, :] = total
    lane = lax.broadcasted_iota(jnp.int32, (1, SLOTS), 1)
    scale = (lane < counts[b]).astype(F32) * (32.0 * force_norm)
    weight = weights[0:1, :]
    for d in range(3):
        push = jnp.sum(acc[d].T, axis=0, keepdims=True)
        drag = jnp.sum(acc[3 + d].T, axis=0, keepdims=True)
        still = near_base[0, d : d + 1, :] + far_base[0, d : d + 1, :]
        out[d, pl.ds(b, 1), :] = (push + weight * (still - viscosity * drag)) * scale


def both_ways(value):
    count = lax.axis_size("slab")
    up = [(i, (i + 1) % count) for i in range(count)]
    down = [(j, i) for i, j in up]
    return lax.ppermute(value, "slab", up), lax.ppermute(value, "slab", down)


def cost(pairs, ops):
    work = pairs * SLOTS * SLOTS
    return pl.CostEstimate(flops=work * ops, bytes_accessed=work * 4, transcendentals=work)


def limit(mib):
    return pltpu.CompilerParams(vmem_limit_bytes=mib << 20)


def per_device(particles, counts, partners):
    layers, cols = lax.axis_size("z"), lax.axis_size("x")
    own, block = pl.pallas_call(
        prepare_kernel,
        out_shape=(shape(BINS, ROWS, SLOTS), shape(layers, BINS, ROWS, SLOTS)),
        in_specs=[SMEM, VMEM],
        out_specs=(VMEM, VMEM),
        compiler_params=limit(8),
        name="prepare",
    )(counts, particles)
    up, down = both_ways(own)
    column = lax.all_to_all(block, "z", 0, 0, tiled=True)
    tall, acc, acc3 = (pltpu.VMEM(dims, F32) for dims in ((SLOTS, ROWS), (SLOTS, SLOTS), (3, SLOTS, SLOTS)))
    tile = pl.BlockSpec((1, ROWS, SLOTS), lambda b: (b, 0, 0))
    links = pl.BlockSpec((LINKS, ROWS, SLOTS), lambda b: (b, 0, 0))
    near_pairs = pl.BlockSpec((1, 3, SLOTS, SLOTS), lambda b: (b, 0, 0, 0))
    far_pairs = pl.BlockSpec((1, LINKS, SLOTS, SLOTS), lambda b: (b, 0, 0, 0))
    row = pl.BlockSpec((1, 1, SLOTS), lambda b: (b, 0, 0))
    vector = pl.BlockSpec((1, 3, SLOTS), lambda b: (b, 0, 0))
    part, near_factors, near_base = pl.pallas_call(
        near_kernel,
        grid=(BINS,),
        out_shape=(shape(BINS, 1, SLOTS), shape(BINS, 3, SLOTS, SLOTS), shape(BINS, 3, SLOTS)),
        in_specs=[tile] * 3,
        out_specs=(row, near_pairs, vector),
        scratch_shapes=[tall, acc, acc3],
        cost_estimate=cost(3 * BINS, 60),
        compiler_params=limit(8),
        name="near",
    )(own, up, down)
    column, part, near_factors, near_base = lax.optimization_barrier((column, part, near_factors, near_base))
    near = lax.all_to_all(jnp.broadcast_to(column[None], (cols,) + column.shape), "x", 0, 0, tiled=True)
    near = near.reshape(-1, ROWS, SLOTS)
    far = lax.ppermute(near, "core", [(0, 1), (1, 0)])
    density, mine, block, members = pl.pallas_call(
        partner_density_kernel,
        out_shape=(
            shape(BINS, SLOTS),
            shape(BINS, SLOTS),
            shape(layers * cols, BINS, SLOTS),
            shape(BINS * LINKS, ROWS, SLOTS),
        ),
        in_specs=[SMEM, SMEM, VMEM, VMEM, ANY, ANY],
        out_specs=(VMEM,) * 4,
        scratch_shapes=[tall, acc, pltpu.SemaphoreType.DMA((BINS * LINKS,))],
        cost_estimate=cost(LINKS * BINS, 20),
        compiler_params=limit(8),
        name="partner_density",
    )(partners, counts, own, part, near, far)
    mine_up, mine_down = both_ways(mine)
    inverse = lax.all_to_all(block, ("z", "x"), 0, 0, tiled=True)
    far_factors, far_base = pl.pallas_call(
        factor_kernel,
        grid=(BINS,),
        out_shape=(shape(BINS, LINKS, SLOTS, SLOTS), shape(BINS, 3, SLOTS)),
        in_specs=[tile, links],
        out_specs=(far_pairs, vector),
        scratch_shapes=[tall, acc3],
        cost_estimate=cost(LINKS * BINS, 40),
        compiler_params=limit(8),
        name="factor",
    )(own, members)
    inverse, far_base, mine_up, mine_down = lax.optimization_barrier((inverse, far_base, mine_up, mine_down))
    inverse = lax.all_gather(inverse.reshape(-1, SLOTS), "core", axis=0, tiled=True)
    acceleration = pl.pallas_call(
        force_kernel,
        grid=(BINS,),
        out_shape=shape(3, BINS, SLOTS),
        in_specs=[SMEM, SMEM, tile, tile, tile, links, near_pairs, far_pairs, vector, vector] + [VMEM] * 4,
        out_specs=pl.BlockSpec((3, BINS, SLOTS), lambda b: (0, 0, 0)),
        scratch_shapes=[pltpu.VMEM((16, SLOTS), F32), tall, pltpu.VMEM((6, SLOTS, SLOTS), F32)],
        cost_estimate=cost(COUNT * BINS, 20),
        compiler_params=limit(8),
        name="force",
    )(
        partners,
        counts,
        own,
        up,
        down,
        members,
        near_factors,
        far_factors,
        near_base,
        far_base,
        mine,
        mine_up,
        mine_down,
        inverse,
    )
    return density, acceleration


def solution(mesh):
    grid = Mesh(mesh.devices.reshape(mesh.shape["slab"], 16, 4, 2), ("slab", "z", "x", "core"))
    axes = ("slab", "z", "x", "core")
    return jax.shard_map(
        per_device,
        mesh=grid,
        in_specs=(P(None, axes, None), P(axes), P(axes, None)),
        out_specs=(P(axes, None), P(None, axes, None)),
        check_vma=False,
    )
```

```python
import jax
import jax.numpy as jnp
from jax import lax
from jax.experimental import pallas as pl
from jax.experimental.pallas import tpu as pltpu
from jax.sharding import Mesh, PartitionSpec as P

weight_norm = 21.0 / (16.0 * 3.141592653589793)
force_norm = 105.0 / (16.0 * 3.141592653589793)
viscosity = 0.25

BINS = 4
LINKS = 8
SLOTS = 128
ROWS = 8
COUNT = 3 + LINKS
CHUNKS = SLOTS // 8
F32 = jnp.float32
VMEM = pl.BlockSpec(memory_space=pltpu.MemorySpace.VMEM)
SMEM = pl.BlockSpec(memory_space=pltpu.MemorySpace.SMEM)
HBM = pl.BlockSpec(memory_space=pltpu.MemorySpace.HBM)


def shape(*dims):
    return jax.ShapeDtypeStruct(dims, F32)


def root(square):
    return square * lax.rsqrt(jnp.maximum(square, 1e-36))


def columns(tall, c, rows):
    cols = tall[c * 8 : c * 8 + 8, :]
    return [jnp.broadcast_to(cols[:, r : r + 1], (8, SLOTS)) for r in rows]


def density_terms(tall, others, acc):
    for c in range(CHUNKS):
        xi, yi, zi, hi = columns(tall, c, (0, 1, 2, 6))
        inv = 0.5 / hi
        total = jnp.zeros((8, SLOTS), F32)
        for row in others:
            dx = xi - row(0)
            dy = yi - row(1)
            dz = zi - row(2)
            s = jnp.maximum(1.0 - root(dx * dx + dy * dy + dz * dz) * inv, 0.0)
            s2 = s * s
            total = total + (s2 * s2) * (5.0 - 4.0 * s) * row(7)
        acc[c * 8 : c * 8 + 8, :] = total * (weight_norm / (hi * hi * hi))
    return jnp.sum(acc[...].T, axis=0, keepdims=True)


def reader(ref, *index):
    return lambda r: ref[(*index, pl.ds(r, 8, stride=0), slice(None))]


def prepare_kernel(counts_in, particles_in, own, block, counts, particles, sems):
    fetches = (
        pltpu.make_async_copy(counts_in, counts, sems.at[0]),
        pltpu.make_async_copy(particles_in, particles, sems.at[1]),
    )
    for fetch in fetches:
        fetch.start()
    for fetch in fetches:
        fetch.wait()
    lane = lax.broadcasted_iota(jnp.int32, (1, SLOTS), 1)
    for b in range(BINS):
        filled = (lane < counts[b]).astype(F32)
        for r in range(ROWS):
            row = particles[r, b : b + 1, :]
            own[b, r : r + 1, :] = row * filled if r == 7 else row
        tile = own[b]
        for copy in range(block.shape[0]):
            block[copy, b] = tile


def factor_terms(b, tall, others, store, acc):
    for c in range(CHUNKS):
        xi, yi, zi, hi = columns(tall, c, (0, 1, 2, 6))
        ax = jnp.zeros((8, SLOTS), F32)
        ay, az = ax, ax
        for j, row in enumerate(others):
            dx = xi - row(0)
            dy = yi - row(1)
            dz = zi - row(2)
            inv = 1.0 / (hi + row(6))
            s = jnp.maximum(1.0 - root(dx * dx + dy * dy + dz * dz) * inv, 0.0) * inv
            factor = (s * s * s) * (inv * inv) * row(7)
            store[b, j, c * 8 : c * 8 + 8, :] = factor
            ax = ax + factor * dx
            ay = ay + factor * dy
            az = az + factor * dz
        for d, total in enumerate((ax, ay, az)):
            acc[d, c * 8 : c * 8 + 8, :] = total
    return [jnp.sum(acc[d].T, axis=0, keepdims=True) for d in range(3)]


def near_kernel(own, up, down, part, factors, base, tall, acc, acc3):
    def per_bin(b, carry):
        tall[...] = own[b].T
        others = [reader(ref, b) for ref in (own, up, down)]
        part[pl.ds(b, 1), :] = density_terms(tall, others, acc)
        for d, total in enumerate(factor_terms(b, tall, others, factors, acc3)):
            base[b, d : d + 1, :] = total
        return carry

    lax.fori_loop(0, BINS, per_bin, 0)


def partner_density_kernel(partners, counts, own, part, near, far, den_out, inv_out, block, members, tall, acc):
    me = lax.axis_index("core")

    def per_bin(b, carry):
        for k in range(LINKS):
            bin_id = partners[b, k]
            index = (((bin_id >> 3) & 3) * 16 + (bin_id >> 5)) * BINS + (bin_id & 3)
            mine = ((bin_id >> 2) & 1) == me
            members[b * LINKS + k] = jnp.where(mine, near[index], far[index])
        tall[...] = own[b].T
        far_part = density_terms(tall, [reader(members, b * LINKS + k) for k in range(LINKS)], acc)
        raw = part[pl.ds(b, 1), :] + far_part
        lane = lax.broadcasted_iota(jnp.int32, (1, SLOTS), 1)
        filled = (lane < counts[b]).astype(F32)
        den_out[pl.ds(b, 1), :] = filled * raw
        inv_out[pl.ds(b, 1), :] = 1.0 / (filled * raw + (1.0 - filled))
        return carry

    lax.fori_loop(0, BINS, per_bin, 0)
    inverse = inv_out[...]
    for copy in range(block.shape[0]):
        block[copy] = inverse


def factor_kernel(own, members, factors, base, tall, acc3):
    def per_bin(b, carry):
        tall[...] = own[b].T
        others = [reader(members, b * LINKS + k) for k in range(LINKS)]
        for d, total in enumerate(factor_terms(b, tall, others, factors, acc3)):
            base[b, d : d + 1, :] = total
        return carry

    lax.fori_loop(0, BINS, per_bin, 0)


def force_kernel(
    partners,
    counts,
    own,
    up,
    down,
    members,
    near_factors,
    far_factors,
    near_base,
    far_base,
    mine,
    mine_up,
    mine_down,
    inverse,
    out,
    weights,
    tall,
    acc,
):
    def per_bin(b, carry):
        for j, ref in enumerate((mine, mine_up, mine_down)):
            weights[j : j + 1, :] = ref[pl.ds(b, 1), :]
        for k in range(LINKS):
            bin_id = partners[b, k]
            at = ((bin_id >> 2) & 1) * 256 + (bin_id >> 3) * BINS + (bin_id & 3)
            weights[3 + k : 4 + k, :] = inverse[pl.ds(at, 1), :]
        tall[...] = own[b].T
        others = [(reader(ref, b), near_factors, j) for j, ref in enumerate((own, up, down))]
        others += [(reader(members, b * LINKS + k), far_factors, k) for k in range(LINKS)]
        for c in range(CHUNKS):
            xi, yi, zi, ui, vi, wi = columns(tall, c, range(6))
            ax = jnp.zeros((8, SLOTS), F32)
            ay, az, bx, by, bz = (ax,) * 5
            for j, (row, factors, at) in enumerate(others):
                factor = factors[b, at, c * 8 : c * 8 + 8, :] * weights[pl.ds(j, 8, stride=0), :]
                ax = ax + factor * (xi - row(0))
                ay = ay + factor * (yi - row(1))
                az = az + factor * (zi - row(2))
                bx = bx + factor * (ui - row(3))
                by = by + factor * (vi - row(4))
                bz = bz + factor * (wi - row(5))
            for d, total in enumerate((ax, ay, az, bx, by, bz)):
                acc[d, c * 8 : c * 8 + 8, :] = total
        lane = lax.broadcasted_iota(jnp.int32, (1, SLOTS), 1)
        scale = (lane < counts[b]).astype(F32) * (32.0 * force_norm)
        weight = weights[0:1, :]
        for d in range(3):
            push = jnp.sum(acc[d].T, axis=0, keepdims=True)
            drag = jnp.sum(acc[3 + d].T, axis=0, keepdims=True)
            still = near_base[b, d : d + 1, :] + far_base[b, d : d + 1, :]
            out[d, pl.ds(b, 1), :] = (push + weight * (still - viscosity * drag)) * scale
        return carry

    lax.fori_loop(0, BINS, per_bin, 0)


def both_ways(value):
    count = lax.axis_size("slab")
    up = [(i, (i + 1) % count) for i in range(count)]
    down = [(j, i) for i, j in up]
    return lax.ppermute(value, "slab", up), lax.ppermute(value, "slab", down)


def cost(pairs, ops):
    work = pairs * SLOTS * SLOTS
    return pl.CostEstimate(flops=work * ops, bytes_accessed=work * 4, transcendentals=work)


def limit(mib):
    return pltpu.CompilerParams(vmem_limit_bytes=mib << 20)


def per_device(particles, counts, partners):
    layers, cols = lax.axis_size("z"), lax.axis_size("x")
    own, block = pl.pallas_call(
        prepare_kernel,
        out_shape=(shape(BINS, ROWS, SLOTS), shape(layers, BINS, ROWS, SLOTS)),
        in_specs=[HBM, HBM],
        out_specs=(VMEM, VMEM),
        scratch_shapes=[
            pltpu.SMEM((BINS,), jnp.int32),
            pltpu.VMEM((ROWS, BINS, SLOTS), F32),
            pltpu.SemaphoreType.DMA((2,)),
        ],
        compiler_params=limit(60),
        name="prepare",
    )(counts, particles)
    up, down = both_ways(own)
    column = lax.all_to_all(block, "z", 0, 0, tiled=True)
    tall, acc, acc3 = (pltpu.VMEM(dims, F32) for dims in ((SLOTS, ROWS), (SLOTS, SLOTS), (3, SLOTS, SLOTS)))
    part, near_factors, near_base = pl.pallas_call(
        near_kernel,
        out_shape=(shape(BINS, SLOTS), shape(BINS, 3, SLOTS, SLOTS), shape(BINS, 3, SLOTS)),
        in_specs=[VMEM] * 3,
        out_specs=(VMEM,) * 3,
        scratch_shapes=[tall, acc, acc3],
        cost_estimate=cost(3 * BINS, 60),
        compiler_params=limit(8),
        name="near",
    )(own, up, down)
    column, part, near_factors, near_base = lax.optimization_barrier((column, part, near_factors, near_base))
    near = lax.all_to_all(jnp.broadcast_to(column[None], (cols,) + column.shape), "x", 0, 0, tiled=True)
    near = near.reshape(-1, ROWS, SLOTS)
    far = lax.ppermute(near, "core", [(0, 1), (1, 0)])
    density, mine, block, members = pl.pallas_call(
        partner_density_kernel,
        out_shape=(
            shape(BINS, SLOTS),
            shape(BINS, SLOTS),
            shape(layers * cols, BINS, SLOTS),
            shape(BINS * LINKS, ROWS, SLOTS),
        ),
        in_specs=[SMEM, SMEM] + [VMEM] * 4,
        out_specs=(VMEM,) * 4,
        scratch_shapes=[tall, acc],
        cost_estimate=cost(LINKS * BINS, 20),
        compiler_params=limit(8),
        name="partner_density",
    )(partners, counts, own, part, near, far)
    mine_up, mine_down = both_ways(mine)
    inverse = lax.all_to_all(block, ("z", "x"), 0, 0, tiled=True)
    far_factors, far_base = pl.pallas_call(
        factor_kernel,
        out_shape=(shape(BINS, LINKS, SLOTS, SLOTS), shape(BINS, 3, SLOTS)),
        in_specs=[VMEM] * 2,
        out_specs=(VMEM,) * 2,
        scratch_shapes=[tall, acc3],
        cost_estimate=cost(LINKS * BINS, 40),
        compiler_params=limit(8),
        name="factor",
    )(own, members)
    inverse, far_base, mine_up, mine_down = lax.optimization_barrier((inverse, far_base, mine_up, mine_down))
    inverse = lax.all_gather(inverse.reshape(-1, SLOTS), "core", axis=0, tiled=True)
    acceleration = pl.pallas_call(
        force_kernel,
        out_shape=shape(3, BINS, SLOTS),
        in_specs=[SMEM, SMEM] + [VMEM] * 12,
        out_specs=VMEM,
        scratch_shapes=[pltpu.VMEM((16, SLOTS), F32), tall, pltpu.VMEM((6, SLOTS, SLOTS), F32)],
        cost_estimate=cost(COUNT * BINS, 20),
        compiler_params=limit(8),
        name="force",
    )(
        partners,
        counts,
        own,
        up,
        down,
        members,
        near_factors,
        far_factors,
        near_base,
        far_base,
        mine,
        mine_up,
        mine_down,
        inverse,
    )
    return density, acceleration


def solution(mesh):
    grid = Mesh(mesh.devices.reshape(mesh.shape["slab"], 16, 4, 2), ("slab", "z", "x", "core"))
    axes = ("slab", "z", "x", "core")
    return jax.shard_map(
        per_device,
        mesh=grid,
        in_specs=(P(None, axes, None), P(axes), P(axes, None)),
        out_specs=(P(axes, None), P(None, axes, None)),
        check_vma=False,
    )
```

```python
import jax
import jax.numpy as jnp
from jax import lax
from jax.experimental import pallas as pl
from jax.experimental.pallas import tpu as pltpu
from jax.sharding import Mesh, PartitionSpec as P

weight_norm = 21.0 / (16.0 * 3.141592653589793)
force_norm = 105.0 / (16.0 * 3.141592653589793)
viscosity = 0.25

BINS = 4
LINKS = 8
SLOTS = 128
ROWS = 8
COUNT = 3 + LINKS
CHUNKS = SLOTS // 8
F32 = jnp.float32
VMEM = pl.BlockSpec(memory_space=pltpu.MemorySpace.VMEM)
SMEM = pl.BlockSpec(memory_space=pltpu.MemorySpace.SMEM)
HBM = pl.BlockSpec(memory_space=pltpu.MemorySpace.HBM)


def shape(*dims):
    return jax.ShapeDtypeStruct(dims, F32)


def root(square):
    return square * lax.rsqrt(jnp.maximum(square, 1e-36))


def columns(tall, c, rows):
    cols = tall[c * 8 : c * 8 + 8, :]
    return [jnp.broadcast_to(cols[:, r : r + 1], (8, SLOTS)) for r in rows]


def density_terms(tall, others, acc):
    for c in range(CHUNKS):
        xi, yi, zi, hi = columns(tall, c, (0, 1, 2, 6))
        inv = 0.5 / hi
        total = jnp.zeros((8, SLOTS), F32)
        for row in others:
            dx = xi - row(0)
            dy = yi - row(1)
            dz = zi - row(2)
            s = jnp.maximum(1.0 - root(dx * dx + dy * dy + dz * dz) * inv, 0.0)
            s2 = s * s
            total = total + (s2 * s2) * (5.0 - 4.0 * s) * row(7)
        acc[c * 8 : c * 8 + 8, :] = total * (weight_norm / (hi * hi * hi))
    return jnp.sum(acc[...].T, axis=0, keepdims=True)


def reader(ref, *index):
    return lambda r: ref[(*index, pl.ds(r, 8, stride=0), slice(None))]


def prepare_kernel(counts_in, particles_in, own, block, counts, particles, sems):
    fetches = (
        pltpu.make_async_copy(counts_in, counts, sems.at[0]),
        pltpu.make_async_copy(particles_in, particles, sems.at[1]),
    )
    for fetch in fetches:
        fetch.start()
    for fetch in fetches:
        fetch.wait()
    lane = lax.broadcasted_iota(jnp.int32, (1, SLOTS), 1)
    for b in range(BINS):
        filled = (lane < counts[b]).astype(F32)
        for r in range(ROWS):
            row = particles[r, b : b + 1, :]
            own[b, r : r + 1, :] = row * filled if r == 7 else row
        tile = own[b]
        for copy in range(block.shape[0]):
            block[copy, b] = tile


def factor_terms(b, tall, others, store, acc):
    for c in range(CHUNKS):
        xi, yi, zi, hi = columns(tall, c, (0, 1, 2, 6))
        ax = jnp.zeros((8, SLOTS), F32)
        ay, az = ax, ax
        for j, row in enumerate(others):
            dx = xi - row(0)
            dy = yi - row(1)
            dz = zi - row(2)
            inv = 1.0 / (hi + row(6))
            s = jnp.maximum(1.0 - root(dx * dx + dy * dy + dz * dz) * inv, 0.0) * inv
            factor = (s * s * s) * (inv * inv) * row(7)
            store[b, j, c * 8 : c * 8 + 8, :] = factor
            ax = ax + factor * dx
            ay = ay + factor * dy
            az = az + factor * dz
        for d, total in enumerate((ax, ay, az)):
            acc[d, c * 8 : c * 8 + 8, :] = total
    return [jnp.sum(acc[d].T, axis=0, keepdims=True) for d in range(3)]


def near_kernel(own, up, down, part, factors, base, tall, acc, acc3):
    def per_bin(b, carry):
        tall[...] = own[b].T
        others = [reader(ref, b) for ref in (own, up, down)]
        part[pl.ds(b, 1), :] = density_terms(tall, others, acc)
        for d, total in enumerate(factor_terms(b, tall, others, factors, acc3)):
            base[b, d : d + 1, :] = total
        return carry

    lax.fori_loop(0, BINS, per_bin, 0)


def place(bin_id):
    index = (((bin_id >> 3) & 3) * 16 + (bin_id >> 5)) * BINS + (bin_id & 3)
    return index, ((bin_id >> 2) & 1) == lax.axis_index("core")


def add_partners(partners, b, held, wanted, cols, sums):
    for k in range(LINKS):
        index, local = place(partners[b, k])

        @pl.when(local == wanted)
        def _():
            row = reader(held, index)
            for c in range(CHUNKS):
                part = slice(c * 8, c * 8 + 8)
                dx = cols[b, 0, part, :] - row(0)
                dy = cols[b, 1, part, :] - row(1)
                dz = cols[b, 2, part, :] - row(2)
                s = jnp.maximum(1.0 - root(dx * dx + dy * dy + dz * dz) * cols[b, 3, part, :], 0.0)
                s2 = s * s
                sums[b, part, :] = sums[b, part, :] + (s2 * s2) * (5.0 - 4.0 * s) * row(7)


def local_density_kernel(partners, own, near, cols, sums, tall):
    def per_bin(b, carry):
        tall[...] = own[b].T
        for c in range(CHUNKS):
            part = slice(c * 8, c * 8 + 8)
            xi, yi, zi, hi = columns(tall, c, (0, 1, 2, 6))
            for r, value in enumerate((xi, yi, zi, 0.5 / hi)):
                cols[b, r, part, :] = value
            sums[b, part, :] = jnp.zeros((8, SLOTS), F32)
        add_partners(partners, b, near, True, cols, sums)
        return carry

    lax.fori_loop(0, BINS, per_bin, 0)


def partner_density_kernel(partners, own, part, near, far, cols, start, den_out, inv_out, block, members, sums):
    def per_bin(b, carry):
        for k in range(LINKS):
            index, local = place(partners[b, k])
            members[b * LINKS + k] = jnp.where(local, near[index], far[index])
        sums[b] = start[b]
        add_partners(partners, b, far, False, cols, sums)
        width = own[b, 6:7, :]
        far_part = jnp.sum(sums[b].T, axis=0, keepdims=True) * (weight_norm / (width * width * width))
        raw = part[pl.ds(b, 1), :] + far_part
        filled = (own[b, 7:8, :] > 0.0).astype(F32)
        den_out[pl.ds(b, 1), :] = filled * raw
        inv_out[pl.ds(b, 1), :] = 1.0 / (filled * raw + (1.0 - filled))
        return carry

    lax.fori_loop(0, BINS, per_bin, 0)
    inverse = inv_out[...]
    for copy in range(block.shape[0]):
        block[copy] = inverse


def factor_kernel(own, members, density, den_out, factors, base, tall, acc3):
    den_out[...] = density[...]

    def per_bin(b, carry):
        tall[...] = own[b].T
        others = [reader(members, b * LINKS + k) for k in range(LINKS)]
        for d, total in enumerate(factor_terms(b, tall, others, factors, acc3)):
            base[b, d : d + 1, :] = total
        return carry

    lax.fori_loop(0, BINS, per_bin, 0)


def force_kernel(
    partners,
    own,
    up,
    down,
    members,
    near_factors,
    far_factors,
    near_base,
    far_base,
    mine,
    mine_up,
    mine_down,
    inverse,
    out,
    weights,
    tall,
    acc,
):
    def per_bin(b, carry):
        for j, ref in enumerate((mine, mine_up, mine_down)):
            weights[j : j + 1, :] = ref[pl.ds(b, 1), :]
        for k in range(LINKS):
            bin_id = partners[b, k]
            at = ((bin_id >> 2) & 1) * 256 + (bin_id >> 3) * BINS + (bin_id & 3)
            weights[3 + k : 4 + k, :] = inverse[pl.ds(at, 1), :]
        tall[...] = own[b].T
        others = [(reader(ref, b), near_factors, j) for j, ref in enumerate((own, up, down))]
        others += [(reader(members, b * LINKS + k), far_factors, k) for k in range(LINKS)]
        for c in range(CHUNKS):
            xi, yi, zi, ui, vi, wi = columns(tall, c, range(6))
            ax = jnp.zeros((8, SLOTS), F32)
            ay, az, bx, by, bz = (ax,) * 5
            for j, (row, factors, at) in enumerate(others):
                factor = factors[b, at, c * 8 : c * 8 + 8, :] * weights[pl.ds(j, 8, stride=0), :]
                ax = ax + factor * (xi - row(0))
                ay = ay + factor * (yi - row(1))
                az = az + factor * (zi - row(2))
                bx = bx + factor * (ui - row(3))
                by = by + factor * (vi - row(4))
                bz = bz + factor * (wi - row(5))
            for d, total in enumerate((ax, ay, az, bx, by, bz)):
                acc[d, c * 8 : c * 8 + 8, :] = total
        scale = (own[b, 7:8, :] > 0.0).astype(F32) * (32.0 * force_norm)
        weight = weights[0:1, :]
        for d in range(3):
            push = jnp.sum(acc[d].T, axis=0, keepdims=True)
            drag = jnp.sum(acc[3 + d].T, axis=0, keepdims=True)
            still = near_base[b, d : d + 1, :] + far_base[b, d : d + 1, :]
            out[d, pl.ds(b, 1), :] = (push + weight * (still - viscosity * drag)) * scale
        return carry

    lax.fori_loop(0, BINS, per_bin, 0)


def both_ways(value):
    count = lax.axis_size("slab")
    up = [(i, (i + 1) % count) for i in range(count)]
    down = [(j, i) for i, j in up]
    return lax.ppermute(value, "slab", up), lax.ppermute(value, "slab", down)


def cost(pairs, ops):
    work = pairs * SLOTS * SLOTS
    return pl.CostEstimate(flops=work * ops, bytes_accessed=work * 4, transcendentals=work)


def limit(mib):
    return pltpu.CompilerParams(vmem_limit_bytes=mib << 20)


def per_device(particles, counts, partners):
    layers, cols_count = lax.axis_size("z"), lax.axis_size("x")
    own, block = pl.pallas_call(
        prepare_kernel,
        out_shape=(shape(BINS, ROWS, SLOTS), shape(layers, BINS, ROWS, SLOTS)),
        in_specs=[HBM, HBM],
        out_specs=(VMEM, VMEM),
        scratch_shapes=[
            pltpu.SMEM((BINS,), jnp.int32),
            pltpu.VMEM((ROWS, BINS, SLOTS), F32),
            pltpu.SemaphoreType.DMA((2,)),
        ],
        compiler_params=limit(60),
        name="prepare",
    )(counts, particles)
    up, down = both_ways(own)
    column = lax.all_to_all(block, "z", 0, 0, tiled=True)
    tall, acc, acc3 = (pltpu.VMEM(dims, F32) for dims in ((SLOTS, ROWS), (SLOTS, SLOTS), (3, SLOTS, SLOTS)))
    part, near_factors, near_base = pl.pallas_call(
        near_kernel,
        out_shape=(shape(BINS, SLOTS), shape(BINS, 3, SLOTS, SLOTS), shape(BINS, 3, SLOTS)),
        in_specs=[VMEM] * 3,
        out_specs=(VMEM,) * 3,
        scratch_shapes=[tall, acc, acc3],
        cost_estimate=cost(3 * BINS, 60),
        compiler_params=limit(8),
        name="near",
    )(own, up, down)
    column, part, near_factors, near_base = lax.optimization_barrier((column, part, near_factors, near_base))
    near = lax.all_to_all(jnp.broadcast_to(column[None], (cols_count,) + column.shape), "x", 0, 0, tiled=True)
    near = near.reshape(-1, ROWS, SLOTS)
    far = lax.ppermute(near, "core", [(0, 1), (1, 0)])
    cols, sums = pl.pallas_call(
        local_density_kernel,
        out_shape=(shape(BINS, 4, SLOTS, SLOTS), shape(BINS, SLOTS, SLOTS)),
        in_specs=[SMEM] + [VMEM] * 2,
        out_specs=(VMEM,) * 2,
        scratch_shapes=[tall],
        cost_estimate=cost(LINKS * BINS, 20),
        compiler_params=limit(8),
        name="local_density",
    )(partners, own, near)
    density, mine, block, members = pl.pallas_call(
        partner_density_kernel,
        out_shape=(
            shape(BINS, SLOTS),
            shape(BINS, SLOTS),
            shape(layers * cols_count, BINS, SLOTS),
            shape(BINS * LINKS, ROWS, SLOTS),
        ),
        in_specs=[SMEM] + [VMEM] * 6,
        out_specs=(VMEM,) * 4,
        scratch_shapes=[pltpu.VMEM((BINS, SLOTS, SLOTS), F32)],
        cost_estimate=cost(LINKS * BINS, 20),
        compiler_params=limit(8),
        name="partner_density",
    )(partners, own, part, near, far, cols, sums)
    mine_up, mine_down = both_ways(mine)
    inverse = lax.all_to_all(block, ("z", "x"), 0, 0, tiled=True)
    density, far_factors, far_base = pl.pallas_call(
        factor_kernel,
        out_shape=(
            shape(BINS, SLOTS),
            shape(BINS, LINKS, SLOTS, SLOTS),
            shape(BINS, 3, SLOTS),
        ),
        in_specs=[VMEM] * 3,
        out_specs=(VMEM,) * 3,
        scratch_shapes=[tall, acc3],
        cost_estimate=cost(LINKS * BINS, 40),
        compiler_params=limit(8),
        name="factor",
    )(own, members, density)
    inverse, far_base, mine_up, mine_down = lax.optimization_barrier((inverse, far_base, mine_up, mine_down))
    inverse = lax.all_gather(inverse.reshape(-1, SLOTS), "core", axis=0, tiled=True)
    acceleration = pl.pallas_call(
        force_kernel,
        out_shape=shape(3, BINS, SLOTS),
        in_specs=[SMEM] + [VMEM] * 12,
        out_specs=VMEM,
        scratch_shapes=[pltpu.VMEM((16, SLOTS), F32), tall, pltpu.VMEM((6, SLOTS, SLOTS), F32)],
        cost_estimate=cost(COUNT * BINS, 20),
        compiler_params=limit(8),
        name="force",
    )(
        partners,
        own,
        up,
        down,
        members,
        near_factors,
        far_factors,
        near_base,
        far_base,
        mine,
        mine_up,
        mine_down,
        inverse,
    )
    return density, acceleration


def solution(mesh):
    grid = Mesh(mesh.devices.reshape(mesh.shape["slab"], 16, 4, 2), ("slab", "z", "x", "core"))
    axes = ("slab", "z", "x", "core")
    return jax.shard_map(
        per_device,
        mesh=grid,
        in_specs=(P(None, axes, None), P(axes), P(axes, None)),
        out_specs=(P(axes, None), P(None, axes, None)),
        check_vma=False,
    )
```

```python
import jax
import jax.numpy as jnp
from jax import lax
from jax.experimental import pallas as pl
from jax.experimental.pallas import tpu as pltpu
from jax.sharding import Mesh, PartitionSpec as P

weight_norm = 21.0 / (16.0 * 3.141592653589793)
force_norm = 105.0 / (16.0 * 3.141592653589793)
viscosity = 0.25

BINS = 4
LINKS = 8
SLOTS = 128
ROWS = 8
COUNT = 3 + LINKS
CHUNKS = SLOTS // 8
F32 = jnp.float32
VMEM = pl.BlockSpec(memory_space=pltpu.MemorySpace.VMEM)
SMEM = pl.BlockSpec(memory_space=pltpu.MemorySpace.SMEM)
HBM = pl.BlockSpec(memory_space=pltpu.MemorySpace.HBM)


def shape(*dims):
    return jax.ShapeDtypeStruct(dims, F32)


def root(square):
    return square * lax.rsqrt(jnp.maximum(square, 1e-36))


def columns(tall, c, rows):
    cols = tall[c * 8 : c * 8 + 8, :]
    return [jnp.broadcast_to(cols[:, r : r + 1], (8, SLOTS)) for r in rows]


def density_terms(tall, others, acc):
    for c in range(CHUNKS):
        xi, yi, zi, hi = columns(tall, c, (0, 1, 2, 6))
        inv = 0.5 / hi
        total = jnp.zeros((8, SLOTS), F32)
        for row in others:
            dx = xi - row(0)
            dy = yi - row(1)
            dz = zi - row(2)
            s = jnp.maximum(1.0 - root(dx * dx + dy * dy + dz * dz) * inv, 0.0)
            s2 = s * s
            total = total + (s2 * s2) * (5.0 - 4.0 * s) * row(7)
        acc[c * 8 : c * 8 + 8, :] = total * (weight_norm / (hi * hi * hi))
    return jnp.sum(acc[...].T, axis=0, keepdims=True)


def reader(ref, *index):
    return lambda r: ref[(*index, pl.ds(r, 8, stride=0), slice(None))]


def prepare_kernel(counts_in, particles_in, own, block, counts, particles, sems):
    fetches = (
        pltpu.make_async_copy(counts_in, counts, sems.at[0]),
        pltpu.make_async_copy(particles_in, particles, sems.at[1]),
    )
    for fetch in fetches:
        fetch.start()
    for fetch in fetches:
        fetch.wait()
    lane = lax.broadcasted_iota(jnp.int32, (1, SLOTS), 1)
    for b in range(BINS):
        filled = (lane < counts[b]).astype(F32)
        for r in range(ROWS):
            row = particles[r, b : b + 1, :]
            own[b, r : r + 1, :] = row * filled if r == 7 else row
        tile = own[b]
        for copy in range(block.shape[0]):
            block[copy, b] = tile


def factor_terms(b, tall, others, store, acc):
    for c in range(CHUNKS):
        xi, yi, zi, hi = columns(tall, c, (0, 1, 2, 6))
        ax = jnp.zeros((8, SLOTS), F32)
        ay, az = ax, ax
        for j, row in enumerate(others):
            dx = xi - row(0)
            dy = yi - row(1)
            dz = zi - row(2)
            inv = 1.0 / (hi + row(6))
            s = jnp.maximum(1.0 - root(dx * dx + dy * dy + dz * dz) * inv, 0.0) * inv
            factor = (s * s * s) * (inv * inv) * row(7)
            store[b, j, c * 8 : c * 8 + 8, :] = factor
            ax = ax + factor * dx
            ay = ay + factor * dy
            az = az + factor * dz
        for d, total in enumerate((ax, ay, az)):
            acc[d, c * 8 : c * 8 + 8, :] = total
    return [jnp.sum(acc[d].T, axis=0, keepdims=True) for d in range(3)]


def near_kernel(own, up, down, part, factors, base, tall, acc, acc3):
    def per_bin(b, carry):
        tall[...] = own[b].T
        others = [reader(ref, b) for ref in (own, up, down)]
        part[pl.ds(b, 1), :] = density_terms(tall, others, acc)
        for d, total in enumerate(factor_terms(b, tall, others, factors, acc3)):
            base[b, d : d + 1, :] = total
        return carry

    lax.fori_loop(0, BINS, per_bin, 0)


def place(bin_id):
    index = (((bin_id >> 3) & 3) * 16 + (bin_id >> 5)) * BINS + (bin_id & 3)
    return index, ((bin_id >> 2) & 1) == lax.axis_index("core")


def add_partners(partners, b, held, wanted, cols, sums):
    for k in range(LINKS):
        index, local = place(partners[b, k])

        @pl.when(local == wanted)
        def _():
            row = reader(held, index)
            for c in range(CHUNKS):
                part = slice(c * 8, c * 8 + 8)
                dx = cols[b, 0, part, :] - row(0)
                dy = cols[b, 1, part, :] - row(1)
                dz = cols[b, 2, part, :] - row(2)
                s = jnp.maximum(1.0 - root(dx * dx + dy * dy + dz * dz) * cols[b, 3, part, :], 0.0)
                s2 = s * s
                sums[b, part, :] = sums[b, part, :] + (s2 * s2) * (5.0 - 4.0 * s) * row(7)


def local_density_kernel(partners, own, near, cols, sums, tall):
    def per_bin(b, carry):
        tall[...] = own[b].T
        for c in range(CHUNKS):
            part = slice(c * 8, c * 8 + 8)
            xi, yi, zi, hi = columns(tall, c, (0, 1, 2, 6))
            for r, value in enumerate((xi, yi, zi, 0.5 / hi)):
                cols[b, r, part, :] = value
            sums[b, part, :] = jnp.zeros((8, SLOTS), F32)
        add_partners(partners, b, near, True, cols, sums)
        return carry

    lax.fori_loop(0, BINS, per_bin, 0)


def partner_density_kernel(partners, own, part, near, far, cols, start, den_out, inv_out, block, members, sums):
    def per_bin(b, carry):
        for k in range(LINKS):
            index, local = place(partners[b, k])
            members[b * LINKS + k] = jnp.where(local, near[index], far[index])
        sums[b] = start[b]
        add_partners(partners, b, far, False, cols, sums)
        width = own[b, 6:7, :]
        far_part = jnp.sum(sums[b].T, axis=0, keepdims=True) * (weight_norm / (width * width * width))
        raw = part[pl.ds(b, 1), :] + far_part
        filled = (own[b, 7:8, :] > 0.0).astype(F32)
        den_out[pl.ds(b, 1), :] = filled * raw
        inv_out[pl.ds(b, 1), :] = 1.0 / (filled * raw + (1.0 - filled))
        return carry

    lax.fori_loop(0, BINS, per_bin, 0)
    inverse = inv_out[...]
    for copy in range(block.shape[0]):
        block[copy] = inverse


def factor_kernel(own, members, density, den_out, factors, base, tall, acc3):
    den_out[...] = density[...]

    def per_bin(b, carry):
        tall[...] = own[b].T
        others = [reader(members, b * LINKS + k) for k in range(LINKS)]
        for d, total in enumerate(factor_terms(b, tall, others, factors, acc3)):
            base[b, d : d + 1, :] = total
        return carry

    lax.fori_loop(0, BINS, per_bin, 0)


def force_terms(b, tall, others, acc):
    for c in range(CHUNKS):
        part = slice(c * 8, c * 8 + 8)
        xi, yi, zi, ui, vi, wi = columns(tall, c, range(6))
        ax = jnp.zeros((8, SLOTS), F32)
        ay, az, bx, by, bz = (ax,) * 5
        for row, factors, at, weight in others:
            factor = factors[b, at, part, :] * weight()
            ax = ax + factor * (xi - row(0))
            ay = ay + factor * (yi - row(1))
            az = az + factor * (zi - row(2))
            bx = bx + factor * (ui - row(3))
            by = by + factor * (vi - row(4))
            bz = bz + factor * (wi - row(5))
        for d, total in enumerate((ax, ay, az, bx, by, bz)):
            acc[d, part, :] = total
    return [jnp.sum(acc[d].T, axis=0, keepdims=True) for d in range(6)]


def spread_row(ref, j):
    return lambda: ref[pl.ds(j, 8, stride=0), :]


def near_force_kernel(own, up, down, factors, near_base, far_base, mine, mine_up, mine_down, out, tall, acc):
    def per_bin(b, carry):
        tall[...] = own[b].T
        pairs = ((own, mine), (up, mine_up), (down, mine_down))
        others = [(reader(ref, b), factors, j, spread_row(weight, b)) for j, (ref, weight) in enumerate(pairs)]
        sums = force_terms(b, tall, others, acc)
        weight = mine[pl.ds(b, 1), :]
        for d in range(3):
            still = near_base[b, d : d + 1, :] + far_base[b, d : d + 1, :]
            out[b, d : d + 1, :] = sums[d] + weight * (still - viscosity * sums[3 + d])
        return carry

    lax.fori_loop(0, BINS, per_bin, 0)


def force_kernel(partners, own, members, factors, begun, mine, inverse, out, weights, tall, acc):
    def per_bin(b, carry):
        for k in range(LINKS):
            bin_id = partners[b, k]
            at = ((bin_id >> 2) & 1) * 256 + (bin_id >> 3) * BINS + (bin_id & 3)
            weights[k : k + 1, :] = inverse[pl.ds(at, 1), :]
        tall[...] = own[b].T
        others = [(reader(members, b * LINKS + k), factors, k, spread_row(weights, k)) for k in range(LINKS)]
        sums = force_terms(b, tall, others, acc)
        scale = (own[b, 7:8, :] > 0.0).astype(F32) * (32.0 * force_norm)
        drag = viscosity * mine[pl.ds(b, 1), :]
        for d in range(3):
            out[d, pl.ds(b, 1), :] = (begun[b, d : d + 1, :] + sums[d] - drag * sums[3 + d]) * scale
        return carry

    lax.fori_loop(0, BINS, per_bin, 0)


def both_ways(value):
    count = lax.axis_size("slab")
    up = [(i, (i + 1) % count) for i in range(count)]
    down = [(j, i) for i, j in up]
    return lax.ppermute(value, "slab", up), lax.ppermute(value, "slab", down)


def cost(pairs, ops):
    work = pairs * SLOTS * SLOTS
    return pl.CostEstimate(flops=work * ops, bytes_accessed=work * 4, transcendentals=work)


def limit(mib):
    return pltpu.CompilerParams(vmem_limit_bytes=mib << 20)


def per_device(particles, counts, partners):
    layers, cols_count = lax.axis_size("z"), lax.axis_size("x")
    own, block = pl.pallas_call(
        prepare_kernel,
        out_shape=(shape(BINS, ROWS, SLOTS), shape(layers, BINS, ROWS, SLOTS)),
        in_specs=[HBM, HBM],
        out_specs=(VMEM, VMEM),
        scratch_shapes=[
            pltpu.SMEM((BINS,), jnp.int32),
            pltpu.VMEM((ROWS, BINS, SLOTS), F32),
            pltpu.SemaphoreType.DMA((2,)),
        ],
        compiler_params=limit(60),
        name="prepare",
    )(counts, particles)
    up, down = both_ways(own)
    column = lax.all_to_all(block, "z", 0, 0, tiled=True)
    tall, acc, acc3 = (pltpu.VMEM(dims, F32) for dims in ((SLOTS, ROWS), (SLOTS, SLOTS), (3, SLOTS, SLOTS)))
    part, near_factors, near_base = pl.pallas_call(
        near_kernel,
        out_shape=(shape(BINS, SLOTS), shape(BINS, 3, SLOTS, SLOTS), shape(BINS, 3, SLOTS)),
        in_specs=[VMEM] * 3,
        out_specs=(VMEM,) * 3,
        scratch_shapes=[tall, acc, acc3],
        cost_estimate=cost(3 * BINS, 60),
        compiler_params=limit(8),
        name="near",
    )(own, up, down)
    column, part, near_factors, near_base = lax.optimization_barrier((column, part, near_factors, near_base))
    near = lax.all_to_all(jnp.broadcast_to(column[None], (cols_count,) + column.shape), "x", 0, 0, tiled=True)
    near = near.reshape(-1, ROWS, SLOTS)
    far = lax.ppermute(near, "core", [(0, 1), (1, 0)])
    cols, sums = pl.pallas_call(
        local_density_kernel,
        out_shape=(shape(BINS, 4, SLOTS, SLOTS), shape(BINS, SLOTS, SLOTS)),
        in_specs=[SMEM] + [VMEM] * 2,
        out_specs=(VMEM,) * 2,
        scratch_shapes=[tall],
        cost_estimate=cost(LINKS * BINS, 20),
        compiler_params=limit(8),
        name="local_density",
    )(partners, own, near)
    density, mine, block, members = pl.pallas_call(
        partner_density_kernel,
        out_shape=(
            shape(BINS, SLOTS),
            shape(BINS, SLOTS),
            shape(layers * cols_count, BINS, SLOTS),
            shape(BINS * LINKS, ROWS, SLOTS),
        ),
        in_specs=[SMEM] + [VMEM] * 6,
        out_specs=(VMEM,) * 4,
        scratch_shapes=[pltpu.VMEM((BINS, SLOTS, SLOTS), F32)],
        cost_estimate=cost(LINKS * BINS, 20),
        compiler_params=limit(8),
        name="partner_density",
    )(partners, own, part, near, far, cols, sums)
    mine_up, mine_down = both_ways(mine)
    inverse = lax.all_to_all(block, ("z", "x"), 0, 0, tiled=True)
    density, far_factors, far_base = pl.pallas_call(
        factor_kernel,
        out_shape=(
            shape(BINS, SLOTS),
            shape(BINS, LINKS, SLOTS, SLOTS),
            shape(BINS, 3, SLOTS),
        ),
        in_specs=[VMEM] * 3,
        out_specs=(VMEM,) * 3,
        scratch_shapes=[tall, acc3],
        cost_estimate=cost(LINKS * BINS, 40),
        compiler_params=limit(8),
        name="factor",
    )(own, members, density)
    acc6 = pltpu.VMEM((6, SLOTS, SLOTS), F32)
    begun = pl.pallas_call(
        near_force_kernel,
        out_shape=shape(BINS, 3, SLOTS),
        in_specs=[VMEM] * 9,
        out_specs=VMEM,
        scratch_shapes=[tall, acc6],
        cost_estimate=cost(3 * BINS, 40),
        compiler_params=limit(8),
        name="near_force",
    )(own, up, down, near_factors, near_base, far_base, mine, mine_up, mine_down)
    inverse, begun = lax.optimization_barrier((inverse, begun))
    inverse = lax.all_gather(inverse.reshape(-1, SLOTS), "core", axis=0, tiled=True)
    acceleration = pl.pallas_call(
        force_kernel,
        out_shape=shape(3, BINS, SLOTS),
        in_specs=[SMEM] + [VMEM] * 6,
        out_specs=VMEM,
        scratch_shapes=[pltpu.VMEM((8, SLOTS), F32), tall, acc6],
        cost_estimate=cost(LINKS * BINS, 20),
        compiler_params=limit(8),
        name="force",
    )(partners, own, members, far_factors, begun, mine, inverse)
    return density, acceleration


def solution(mesh):
    grid = Mesh(mesh.devices.reshape(mesh.shape["slab"], 16, 4, 2), ("slab", "z", "x", "core"))
    axes = ("slab", "z", "x", "core")
    return jax.shard_map(
        per_device,
        mesh=grid,
        in_specs=(P(None, axes, None), P(axes), P(axes, None)),
        out_specs=(P(axes, None), P(None, axes, None)),
        check_vma=False,
    )
```
